512 devices in a mesh: batch: 16 (over z), token: 32 (over x, y, core).
Axes of the slice: x: 4, y: 4, z: 16, core: 2. Of those that a mesh axis runs over, the one named last changes fastest.
Arguments:
- tokens: bfloat16 [262144, 768], P(('batch', 'token')), may hold values from -9 to 9
- slot_weight: bfloat16 [768, 1024], replicated, may hold values from -2 to 2
- expert_in: bfloat16 [128, 768, 3072], P('token', None, 'batch'), may hold values from -1.7265625 to 1.7265625
- expert_out: bfloat16 [128, 3072, 768], P('token', 'batch'), may hold values from -0.6484375 to 0.6484375
Outputs:
- mixed: bfloat16 [262144, 768], P(('batch', 'token'))
The draws below stay inside these ranges and needn't reach their ends.
All inputs are finite; a program needn't handle non-finite values.
Results may differ from the reference program's by a relative error of at most 0.023.
Values may be sent and summed in bfloat16 or wider, within the bound.
A program may use at most 64 MiB of HBM per device.

```python
import jax
import jax.numpy as jnp
from jax import lax

D = 768
FF = 3072
EXPERTS = 128
SLOT_EACH = 8
GROUP_TOK = 16384
TOKENS = 262144
SLOTS = 1024
N_BATCH = 16


def draw_tokens(key, part):
    key_main, key_drift = jax.random.split(jax.random.fold_in(key, 3))
    values = jnp.clip(jax.random.normal(key_main, (TOKENS, D), jnp.float32), -4.0, 4.0)
    drift = jnp.clip(jax.random.normal(key_drift, (D,), jnp.float32), -3.0, 3.0)
    position = (jnp.arange(TOKENS) % GROUP_TOK).astype(jnp.float32) / GROUP_TOK
    values = values + (1.5 * position)[:, None] * drift[None, :]
    return values.astype(jnp.bfloat16)


def draw_slot_weight(key, part):
    scale_value = 2.0 / D ** 0.5
    values = jax.random.normal(jax.random.fold_in(key, 5), (D, SLOTS), jnp.float32) * scale_value
    values = jnp.clip(values, -4.0 * scale_value, 4.0 * scale_value)
    return values.astype(jnp.bfloat16)


def steps_of(own_key, extent, cuts, low, top_value):
    def one(dim, parts):
        draws = jax.random.uniform(jax.random.fold_in(jax.random.fold_in(own_key, 6), dim), (parts,), jnp.float32, low / len(cuts), top_value / len(cuts))
        return jnp.repeat(jnp.exp(draws), extent[dim] // parts).reshape((-1,) + (1,) * (len(extent) - dim - 1))

    factor_of = one(*cuts[0])
    for cut in cuts[1:]:
        factor_of = factor_of * one(*cut)
    return factor_of


def gaussian(key, extent, scale, bound, shards=(), kind=jnp.bfloat16):
    level = steps_of(key, extent, shards, -0.22, 0.18) if shards else 1.0
    entries = jax.random.normal(key, extent, jnp.float32) * scale * level
    return jnp.minimum(jnp.maximum(entries, -bound), bound).astype(kind)


def setup_inputs(seed: int = 0) -> dict:
    key_of = jax.random.split(jax.random.key(seed), 5)
    tokens = draw_tokens(jax.random.fold_in(key_of[4], 71), 0)
    slot_weight = draw_slot_weight(jax.random.fold_in(key_of[4], 71), 0)
    expert_in = gaussian(key_of[2], (EXPERTS, D, FF), (8.0 / D ** 0.5), 1.7265625, ((0, 32), (2, 16)))
    expert_out = gaussian(key_of[3], (EXPERTS, FF, D), (6.0 / FF ** 0.5), 0.6484375, ((0, 32), (1, 16)))
    return dict(tokens=tokens, slot_weight=slot_weight, expert_in=expert_in, expert_out=expert_out)


def normalize(rows_in):
    widened = rows_in.astype(jnp.float32)
    scale_row = lax.rsqrt(lax.optimization_barrier(jnp.mean(widened * widened, axis=-1, keepdims=True)) + 1e-06)
    return (widened * scale_row).astype(jnp.bfloat16)

def reference(tokens, slot_weight, expert_in, expert_out):
    groups = tokens.reshape(N_BATCH, GROUP_TOK, D)

    def first_pass(group_rows):
        normed = normalize(group_rows)
        logits = jnp.dot(normed, slot_weight, preferred_element_type=jnp.float32)
        column_max = lax.optimization_barrier(jnp.max(logits, axis=0))
        raised = jnp.exp(logits - column_max[None, :])
        column_sum = lax.optimization_barrier(jnp.sum(raised, axis=0))
        dispatch = raised.astype(jnp.bfloat16)
        slot_sum = jnp.dot(dispatch.T, normed, preferred_element_type=jnp.float32)
        return (slot_sum / column_sum[:, None]).astype(jnp.bfloat16)
    slot_inputs = lax.map(first_pass, groups)
    by_expert = slot_inputs.reshape(N_BATCH, EXPERTS, SLOT_EACH, D).transpose(1, 0, 2, 3)
    by_expert = by_expert.reshape(EXPERTS, N_BATCH * SLOT_EACH, D)

    def run_expert(packed):
        expert_rows, first_w, second_w = packed
        hidden = jnp.dot(expert_rows, first_w, preferred_element_type=jnp.float32)
        hidden = jax.nn.gelu(hidden, approximate=False).astype(jnp.bfloat16)
        blocks = hidden.reshape(N_BATCH * SLOT_EACH, N_BATCH, FF // N_BATCH).astype(jnp.float32)
        weights_blocks = second_w.reshape(N_BATCH, FF // N_BATCH, D).astype(jnp.float32)
        partials = jnp.einsum('rbf,bfd->brd', blocks, weights_blocks).astype(jnp.bfloat16)
        return lax.optimization_barrier(jnp.sum(partials.astype(jnp.float32), axis=0)).astype(jnp.bfloat16)
    expert_results = lax.map(run_expert, (by_expert, expert_in, expert_out))
    slot_outputs = expert_results.reshape(EXPERTS, N_BATCH, SLOT_EACH, D).transpose(1, 0, 2, 3)
    slot_outputs = slot_outputs.reshape(N_BATCH, SLOTS, D)

    def second_pass(packed):
        group_rows, group_outputs = packed
        normed = normalize(group_rows)
        logits = jnp.dot(normed, slot_weight, preferred_element_type=jnp.float32)
        combine = jax.nn.softmax(logits, axis=1).astype(jnp.bfloat16)
        return jnp.dot(combine, group_outputs, preferred_element_type=jnp.float32).astype(jnp.bfloat16)
    mixed = lax.map(second_pass, (groups, slot_outputs))
    return mixed.reshape(TOKENS, D)
```

```python
import functools

import jax
import jax.numpy as jnp
from jax import lax
from jax.experimental import pallas as pl
from jax.experimental.pallas import tpu as pltpu
from jax.sharding import Mesh
from jax.sharding import PartitionSpec as P

GRID = pl.DeviceIdType.MESH
F32 = jnp.float32
BF16 = jnp.bfloat16
LANES = 128


def layer(
    sizes,
    tokens_hbm,
    slot_hbm,
    first_hbm,
    second_hbm,
    mixed_hbm,
    tok,
    wv,
    w1,
    w2,
    nrm,
    lg,
    lo,
    dsp,
    part,
    st,
    rb,
    sr,
    vv,
    xin,
    tt,
    dsl,
    dsr,
    drl,
    drr,
    gg,
    cb,
    rinv,
    outv,
    load_sem,
    out_sem,
    tok_sem,
    st_send,
    st_recv,
    pb_send,
    pb_recv,
    c_send,
    c_recv,
    d_send,
    d_recv,
    e_send,
    e_recv,
    f_send,
    f_recv,
):
    nz, nx, ny = sizes
    z, x, y, c = (lax.axis_index(a) for a in ("z", "x", "y", "c"))
    T, D = tokens_hbm.shape
    S = slot_hbm.shape[1]
    H = S // 2
    E = first_hbm.shape[0]
    chips = nx * ny
    R = S // (2 * chips)
    RE = R // E
    xh_n = nx // 2
    kr = nz // 2
    kl = kr - 1
    me = x * ny + y
    half_rows = R // 2
    sibling = {"c": 1 - c}
    right = {"z": lax.rem(z + 1, nz)}
    left = {"z": lax.rem(z + nz - 1, nz)}

    barrier = pltpu.get_barrier_semaphore()
    peers = 2

    def greet(dev):
        pl.semaphore_signal(barrier, inc=1, device_id=dev, device_id_type=GRID)

    greet(right)
    greet(left)
    for dx in range(nx):
        for dy in range(ny):
            for dc in range(2):
                if dx or dy or dc:
                    greet(
                        {
                            "x": lax.rem(x + dx, nx),
                            "y": lax.rem(y + dy, ny),
                            "c": lax.rem(c + dc, 2),
                        }
                    )
                    peers += 1

    own_cols = pl.ds(pl.multiple_of(c * H, LANES), H)
    other_cols = pl.ds(pl.multiple_of((1 - c) * H, LANES), H)
    loads = [
        pltpu.make_async_copy(tokens_hbm, tok, load_sem.at[0]),
        pltpu.make_async_copy(slot_hbm.at[:, own_cols], wv.at[0], load_sem.at[1]),
        pltpu.make_async_copy(slot_hbm.at[:, other_cols], wv.at[1], load_sem.at[2]),
        pltpu.make_async_copy(first_hbm, w1, load_sem.at[3]),
        pltpu.make_async_copy(second_hbm, w2, load_sem.at[4]),
    ]
    for load in loads:
        load.start()

    chunk = min(256, T)

    loads[0].wait()

    def normalize(i, _):
        rows = pl.ds(pl.multiple_of(i * 64, 64), 64)
        wide = tok[rows, :].astype(F32)
        mean = jnp.mean(wide * wide, axis=-1, keepdims=True)
        nrm[rows, :] = (wide * lax.rsqrt(mean + 1e-6)).astype(BF16)
        return 0

    lax.fori_loop(0, T // 64, normalize, 0)

    pl.semaphore_wait(barrier, peers)

    swap = pltpu.make_async_remote_copy(
        src_ref=nrm.at[pl.ds(0, T)],
        dst_ref=nrm.at[pl.ds(T, T)],
        send_sem=tok_sem.at[0],
        recv_sem=tok_sem.at[1],
        device_id=sibling,
        device_id_type=GRID,
    )
    swap.start()

    loads[1].wait()
    loads[2].wait()
    for i in range(T // chunk):
        rows = pl.ds(i * chunk, chunk)
        lg[rows, :] = jnp.dot(nrm[rows, :], wv[0], preferred_element_type=F32)
        lo[rows, :] = jnp.dot(nrm[rows, :], wv[1], preferred_element_type=F32)
    swap.wait_recv()
    for i in range(T // chunk):
        rows = pl.ds(T + i * chunk, chunk)
        lg[rows, :] = jnp.dot(nrm[rows, :], wv[0], preferred_element_type=F32)

    step_rows = 64

    def highest(i, best):
        rows = pl.ds(pl.multiple_of(i * step_rows, step_rows), step_rows)
        block = lg[rows, :].reshape(step_rows // 8, 8, H)
        return jnp.maximum(best, jnp.max(block, axis=0))

    best = lax.fori_loop(0, 2 * T // step_rows, highest, jnp.full((8, H), -jnp.inf, F32))
    column_max = jnp.max(best, axis=0, keepdims=True)

    def raise_rows(i, total):
        rows = pl.ds(pl.multiple_of(i * step_rows, step_rows), step_rows)
        raised = jnp.exp(lg[rows, :] - column_max)
        dsp[rows, :] = raised.astype(BF16)
        return total + jnp.sum(raised.reshape(step_rows // 8, 8, H), axis=0)

    total = lax.fori_loop(0, 2 * T // step_rows, raise_rows, jnp.zeros((8, H), F32))
    column_sum = jnp.sum(total, axis=0, keepdims=True)
    for j in range(H // LANES):
        cols = slice(j * LANES, (j + 1) * LANES)
        st[j, 0:1, :] = column_max[:, cols]
        st[j, 1:2, :] = column_sum[:, cols]

    def targets():
        for xh in range(xh_n):
            for yt in range(ny):
                for ct in range(2):
                    yield xh, yt, ct, (xh * ny + yt) * 2 + ct

    def to_owner(xh, yt, ct, number, what):
        xt = xh_n * c + xh
        row = number * R
        if what == "stat":
            src, dst = st.at[row // LANES], sr.at[me]
            ssem, rsem = st_send.at[number], st_recv.at[me]
        else:
            src, dst = part.at[pl.ds(row, R)], rb.at[me]
            ssem, rsem = pb_send.at[number], pb_recv.at[me]
        here = (xt == x) & (yt == y) & (ct == c)
        far = pltpu.make_async_remote_copy(
            src_ref=src,
            dst_ref=dst,
            send_sem=ssem,
            recv_sem=rsem,
            device_id={"x": xt, "y": yt, "c": ct},
            device_id_type=GRID,
        )
        near = pltpu.make_async_copy(src, dst, rsem)
        return here, far, near

    def start_owner(*args):
        here, far, near = to_owner(*args)
        pl.when(jnp.logical_not(here))(far.start)
        pl.when(here)(near.start)

    for xh, yt, ct, number in targets():
        start_owner(xh, yt, ct, number, "stat")

    block = ny * 2 * R
    for xh in range(xh_n):
        value = lax.dot_general(
            dsp[:, xh * block : (xh + 1) * block],
            nrm[...],
            (((0,), (0,)), ((), ())),
            preferred_element_type=F32,
        )
        part[xh * block : (xh + 1) * block, :] = value.astype(BF16)
        for yt in range(ny):
            for ct in range(2):
                start_owner(xh, yt, ct, (xh * ny + yt) * 2 + ct, "part")

    def combine_rows(i, _):
        rows = pl.ds(pl.multiple_of(i * 32, 32), 32)
        one, two = lg[rows, :], lo[rows, :]
        top = jnp.maximum(
            jnp.max(one, axis=1, keepdims=True), jnp.max(two, axis=1, keepdims=True)
        )
        one, two = jnp.exp(one - top), jnp.exp(two - top)
        cb[0, rows, :] = one.astype(BF16)
        cb[1, rows, :] = two.astype(BF16)
        weight = jnp.sum(one, axis=1, keepdims=True) + jnp.sum(two, axis=1, keepdims=True)
        rinv[rows, :] = jnp.broadcast_to(1.0 / weight, (32, LANES))
        return 0

    lax.fori_loop(0, T // 32, combine_rows, 0)

    def arrived(buf, sem, q):
        return pltpu.make_async_remote_copy(
            src_ref=buf.at[q],
            dst_ref=buf.at[q],
            send_sem=sem.at[q],
            recv_sem=sem.at[q],
            device_id=sibling,
            device_id_type=GRID,
        )

    for q in range(chips):
        arrived(sr, st_recv, q).wait_recv()
    tops = [sr[q, 0:1, :] for q in range(chips)]
    peak = functools.reduce(jnp.maximum, tops)
    weights = [jnp.exp(t - peak) for t in tops]
    sums = functools.reduce(jnp.add, [w * sr[q, 1:2, :] for q, w in enumerate(weights)])
    vv[...] = jnp.zeros_like(vv)
    for q in range(chips):
        vv[q : q + 1, :] = weights[q] / sums
    vv[...] = jnp.transpose(vv[...])
    offset = lax.rem((lax.rem(x, xh_n) * ny + y) * 2 * R + c * R, LANES)
    scale = vv[pl.ds(pl.multiple_of(offset, R), R), :]
    acc = jnp.zeros((R, D), F32)
    for q in range(chips):
        arrived(rb, pb_recv, q).wait_recv()
        acc = acc + scale[:, q : q + 1] * rb[q].astype(F32)
    xin[0] = acc.astype(BF16)

    def halves(ref, i, h):
        return ref.at[i, pl.ds(h * half_rows, half_rows)]

    def pass_on(slot, h, dev, to):
        return pltpu.make_async_remote_copy(
            src_ref=halves(xin, slot, h),
            dst_ref=halves(xin, to, h),
            send_sem=c_send.at[to, h],
            recv_sem=c_recv.at[to, h],
            device_id=dev,
            device_id_type=GRID,
        )

    for h in range(2):
        pass_on(0, h, right, 1).start()
        if kl:
            pass_on(0, h, left, kr + 1).start()

    loads[3].wait()
    loads[4].wait()

    def experts(a, b):
        rows_a, rows_b = xin[a].astype(F32), xin[b].astype(F32)
        for e in range(E):
            part_e = slice(e * RE, (e + 1) * RE)
            rows = jnp.concatenate([rows_a[part_e], rows_b[part_e]], axis=0).astype(BF16)
            hidden = lax.dot_general(
                rows, w1[e], (((1,), (1,)), ((), ())), preferred_element_type=F32
            )
            hidden = 0.5 * hidden * (1.0 + lax.erf(hidden * (0.5**0.5)))
            terms = jnp.dot(hidden.astype(BF16), w2[e], preferred_element_type=F32)
            tt[a, pl.ds(e * RE, RE), :] = terms[:RE]
            tt[b, pl.ds(e * RE, RE), :] = terms[RE:]

    def gather_step(k, _):
        for h in range(2):
            pass_on(0, h, right, k).wait_recv()

            @pl.when(k < kr)
            def _():
                pass_on(k, h, right, k + 1).start()

            @pl.when(k <= kl)
            def _():
                pass_on(0, h, left, kr + k).wait_recv()

            @pl.when(k < kl)
            def _():
                pass_on(kr + k, h, left, kr + k + 1).start()

        experts(k, jnp.where(k < kr, kr + k, 0))
        return 0

    lax.fori_loop(1, kr + 1, gather_step, 0)

    def hand_back(k, h, way):
        src, dst, dev = ((dsl, drl, left), (dsr, drr, right))[way]
        return pltpu.make_async_remote_copy(
            src_ref=halves(src, k, h),
            dst_ref=halves(dst, k - 1, h),
            send_sem=d_send.at[way, k, h],
            recv_sem=d_recv.at[way, k - 1, h],
            device_id=dev,
            device_id_type=GRID,
        )

    def return_step(i, _):
        k = kr - i
        for h in range(2):
            rows = pl.ds(h * half_rows, half_rows)

            @pl.when(k == kr)
            def _():
                dsl[k, rows, :] = tt[k, rows, :].astype(BF16)

            @pl.when(k < kr)
            def _():
                hand_back(k + 1, h, 0).wait_recv()
                dsl[k, rows, :] = (tt[k, rows, :] + drl[k, rows, :].astype(F32)).astype(BF16)

            hand_back(k, h, 0).start()

            @pl.when(k == kl)
            def _():
                dsr[k, rows, :] = tt[kr + k, rows, :].astype(BF16)

            @pl.when(k < kl)
            def _():
                hand_back(k + 1, h, 1).wait_recv()
                dsr[k, rows, :] = (tt[kr + k, rows, :] + drr[k, rows, :].astype(F32)).astype(BF16)

            @pl.when(k <= kl)
            def _():
                hand_back(k, h, 1).start()

        return 0

    lax.fori_loop(0, kr, return_step, 0)

    own_place = pl.multiple_of((2 * me + c) * R, R)
    value = tt[0]
    for way, buf in ((0, drl), (1, drr)):
        if way == 0 or kl:
            for h in range(2):
                hand_back(1, h, way).wait_recv()
            value = value + buf[0].astype(F32)
    gg[pl.ds(own_place, R), :] = value.astype(BF16)

    def share(j):
        dx, dy = j // ny, lax.rem(j, ny)
        rows = pl.ds(own_place, R)
        return pltpu.make_async_remote_copy(
            src_ref=gg.at[rows],
            dst_ref=gg.at[rows],
            send_sem=e_send.at[j],
            recv_sem=e_recv.at[me],
            device_id={"x": lax.rem(x + dx, nx), "y": lax.rem(y + dy, ny)},
            device_id_type=GRID,
        )

    def relay(q):
        rows = pl.ds(pl.multiple_of((2 * q + c) * R, R), R)
        return pltpu.make_async_remote_copy(
            src_ref=gg.at[rows],
            dst_ref=gg.at[rows],
            send_sem=f_send.at[q],
            recv_sem=f_recv.at[q],
            device_id=sibling,
            device_id_type=GRID,
        )

    def share_came(q):
        rows = pl.ds(pl.multiple_of((2 * q + c) * R, R), R)
        return pltpu.make_async_remote_copy(
            src_ref=gg.at[rows],
            dst_ref=gg.at[rows],
            send_sem=e_send.at[0],
            recv_sem=e_recv.at[q],
            device_id=sibling,
            device_id_type=GRID,
        )

    def relay_came(q):
        rows = pl.ds(pl.multiple_of((2 * q + 1 - c) * R, R), R)
        return pltpu.make_async_remote_copy(
            src_ref=gg.at[rows],
            dst_ref=gg.at[rows],
            send_sem=f_send.at[q],
            recv_sem=f_recv.at[q],
            device_id=sibling,
            device_id_type=GRID,
        )

    def start_share(j, _):
        share(j).start()
        return 0

    def start_relay(j, _):
        dx, dy = j // ny, lax.rem(j, ny)
        q = lax.rem(x + nx - dx, nx) * ny + lax.rem(y + ny - dy, ny)
        share_came(q).wait_recv()
        relay(q).start()
        return 0

    def end_relay(q, _):
        relay_came(q).wait_recv()
        return 0

    lax.fori_loop(1, chips, start_share, 0)
    relay(me).start()
    lax.fori_loop(1, chips, start_relay, 0)
    lax.fori_loop(0, chips, end_relay, 0)

    mine = pl.ds(pl.multiple_of(c * H, H), H)
    rest = pl.ds(pl.multiple_of((1 - c) * H, H), H)
    outs = []
    for i in range(T // chunk):
        rows = pl.ds(i * chunk, chunk)
        mixed = jnp.dot(cb[0, rows, :], gg[mine, :], preferred_element_type=F32)
        mixed = mixed + jnp.dot(cb[1, rows, :], gg[rest, :], preferred_element_type=F32)
        outv[rows, :] = (mixed * rinv[rows, 0:1]).astype(BF16)
        outs.append(pltpu.make_async_copy(outv.at[rows], mixed_hbm.at[rows], out_sem.at[i]))
        outs[-1].start()

    swap.wait_send()
    for xh, yt, ct, number in targets():
        for what in ("stat", "part"):
            here, far, near = to_owner(xh, yt, ct, number, what)
            pl.when(jnp.logical_not(here))(far.wait_send)

    def sent_gather(k, _):
        for h in range(2):
            pass_on(0, h, right, k).wait_send()

            @pl.when(k <= kl)
            def _():
                pass_on(0, h, left, kr + k).wait_send()

            hand_back(k, h, 0).wait_send()

            @pl.when(k <= kl)
            def _():
                hand_back(k, h, 1).wait_send()

        return 0

    def sent_share(j, _):
        share(j).wait_send()
        return 0

    def sent_relay(q, _):
        relay(q).wait_send()
        return 0

    lax.fori_loop(1, kr + 1, sent_gather, 0)
    lax.fori_loop(1, chips, sent_share, 0)
    lax.fori_loop(0, chips, sent_relay, 0)
    for out in outs:
        out.wait()


def body(sizes, tokens, slot_weight, expert_in, expert_out):
    nz, nx, ny = sizes
    first = jnp.swapaxes(expert_in, 1, 2)
    T, D = tokens.shape
    S = slot_weight.shape[1]
    H = S // 2
    chips = nx * ny
    R = S // (2 * chips)
    E, FF = first.shape[:2]
    kr = nz // 2
    vmem = pltpu.VMEM
    dma = pltpu.SemaphoreType.DMA
    anywhere = pl.BlockSpec(memory_space=pl.ANY)
    return pl.pallas_call(
        functools.partial(layer, sizes),
        out_shape=jax.ShapeDtypeStruct((T, D), BF16),
        in_specs=[anywhere] * 4,
        out_specs=anywhere,
        scratch_shapes=[
            vmem((T, D), BF16),
            vmem((2, D, H), BF16),
            vmem((E, FF, D), BF16),
            vmem((E, FF, D), BF16),
            vmem((2 * T, D), BF16),
            vmem((2 * T, H), F32),
            vmem((T, H), F32),
            vmem((2 * T, H), BF16),
            vmem((H, D), BF16),
            vmem((H // LANES, 8, LANES), F32),
            vmem((chips, R, D), BF16),
            vmem((chips, 8, LANES), F32),
            vmem((LANES, LANES), F32),
            vmem((nz, R, D), BF16),
            vmem((nz, R, D), F32),
            vmem((kr + 1, R, D), BF16),
            vmem((kr + 1, R, D), BF16),
            vmem((kr + 1, R, D), BF16),
            vmem((kr + 1, R, D), BF16),
            vmem((S, D), BF16),
            vmem((2, T, H), BF16),
            vmem((T, LANES), F32),
            vmem((T, D), BF16),
            dma((5,)),
            dma((T // min(256, T),)),
            dma((2,)),
            dma((chips,)),
            dma((chips,)),
            dma((chips,)),
            dma((chips,)),
            dma((nz, 2)),
            dma((nz, 2)),
            dma((2, kr + 1, 2)),
            dma((2, kr + 1, 2)),
            dma((chips,)),
            dma((chips,)),
            dma((chips,)),
            dma((chips,)),
        ],
        compiler_params=pltpu.CompilerParams(
            collective_id=0, has_side_effects=True, vmem_limit_bytes=56 * 2**20
        ),
        name="soft_moe",
    )(tokens, slot_weight, first, expert_out)


def build(devices, sizes):
    nz, nx, ny = sizes
    torus = Mesh(devices.reshape(nz, nx, ny, 2), ("z", "x", "y", "c"))
    token = ("x", "y", "c")
    rows = ("z", "x", "y", "c")
    placed = (P(rows, None), P(), P(token, None, "z"), P(token, "z", None))
    return jax.shard_map(
        functools.partial(body, sizes),
        mesh=torus,
        in_specs=placed,
        out_specs=P(rows, None),
        check_vma=False,
    )


def solution(mesh):
    return build(mesh.devices, (mesh.shape["batch"], 4, 4))
```

```python
import functools

import jax
import jax.numpy as jnp
from jax import lax
from jax.experimental import pallas as pl
from jax.experimental.pallas import tpu as pltpu
from jax.sharding import Mesh
from jax.sharding import PartitionSpec as P

GRID = pl.DeviceIdType.MESH
F32 = jnp.float32
BF16 = jnp.bfloat16
LANES = 128
ORDER = (
    "B0", "B1", "G01", "G03", "X01", "G11", "G13", "G04", "G02", "G06", "X02", "L02", "X11", "G14",
    "G12", "G16", "G05", "X05", "G07", "G08", "X07", "L08", "L07", "L05", "X12", "G15", "X15", "L12",
    "L15", "G17", "G18", "X17", "L18", "L17", "L04", "L01", "L06", "L14", "L11", "L16", "L03", "L13",
    "R0", "R1",
)
BATCHES = {1: (1, 3), 2: (2, 4), 5: (5, 6), 7: (7, 8)}


def parent(r, top):
    if r % 3 == 0:
        return r - 3
    return r - 2 if r == top and r % 3 == 2 else r - 1


def layer(
    sizes,
    tokens_hbm,
    slot_hbm,
    first_hbm,
    second_hbm,
    mixed_hbm,
    tok,
    wv,
    w1,
    w2,
    nrm,
    lg,
    lo,
    dsp,
    part,
    st,
    rb,
    sr,
    vv,
    xin,
    tt,
    dsl,
    dsr,
    drl,
    drr,
    gg,
    cb,
    rinv,
    outv,
    total_out,
    load_sem,
    out_sem,
    tok_sem,
    st_send,
    st_recv,
    pb_send,
    pb_recv,
    c_send,
    c_recv,
    d_send,
    d_recv,
    e_send,
    e_recv,
    f_send,
    f_recv,
):
    nz, nx, ny = sizes
    z, x, y, c = (lax.axis_index(a) for a in ("z", "x", "y", "c"))
    T, D = tokens_hbm.shape
    S = slot_hbm.shape[1]
    H = S // 2
    E = first_hbm.shape[0]
    chips = nx * ny
    R = S // (2 * chips)
    RE = R // E
    xh_n = nx // 2
    kr = nz // 2
    kl = kr - 1
    me = x * ny + y
    half_rows = R // 2
    sibling = {"c": 1 - c}
    tops = (kr, kl)

    def along(way, step):
        return {"z": lax.rem(z + (step if way == 0 else nz - step), nz)}

    def halves(ref, i, h):
        return ref.at[i, pl.ds(h * half_rows, half_rows)]

    barrier = pltpu.get_barrier_semaphore()
    steps = sorted({r - parent(r, top) for top in tops for r in range(1, top + 1)})
    reach = sorted({d % nz for step in steps for d in (step, nz - step)})
    peers = len(reach)

    def greet(dev):
        pl.semaphore_signal(barrier, inc=1, device_id=dev, device_id_type=GRID)

    for step in reach:
        greet({"z": lax.rem(z + step, nz)})
    for dx in range(nx):
        for dy in range(ny):
            for dc in range(2):
                if dx or dy or dc:
                    greet(
                        {
                            "x": lax.rem(x + dx, nx),
                            "y": lax.rem(y + dy, ny),
                            "c": lax.rem(c + dc, 2),
                        }
                    )
                    peers += 1

    chunk = T // 2
    own_cols = pl.ds(pl.multiple_of(c * H, LANES), H)
    other_cols = pl.ds(pl.multiple_of((1 - c) * H, LANES), H)
    loads = [
        pltpu.make_async_copy(tokens_hbm.at[pl.ds(0, chunk)], tok.at[pl.ds(0, chunk)], load_sem.at[0]),
        pltpu.make_async_copy(slot_hbm.at[:, own_cols], wv.at[0], load_sem.at[1]),
        pltpu.make_async_copy(slot_hbm.at[:, other_cols], wv.at[1], load_sem.at[2]),
        pltpu.make_async_copy(first_hbm, w1, load_sem.at[3]),
        pltpu.make_async_copy(second_hbm, w2, load_sem.at[4]),
    ]
    later = pl.ds(chunk, chunk)
    loads.insert(1, pltpu.make_async_copy(tokens_hbm.at[later], tok.at[later], load_sem.at[5]))
    for load in loads:
        load.start()

    loads[0].wait()

    def normalize(i, _):
        rows = pl.ds(pl.multiple_of(i * 64, 64), 64)
        wide = tok[rows, :].astype(F32)
        mean = jnp.mean(wide * wide, axis=-1, keepdims=True)
        nrm[rows, :] = (wide * lax.rsqrt(mean + 1e-6)).astype(BF16)
        return 0

    lax.fori_loop(0, chunk // 64, normalize, 0)
    loads[1].wait()
    lax.fori_loop(chunk // 64, T // 64, normalize, 0)

    pl.semaphore_wait(barrier, peers)

    def swap(i):
        return pltpu.make_async_remote_copy(
            src_ref=nrm.at[pl.ds(i * chunk, chunk)],
            dst_ref=nrm.at[pl.ds(T + i * chunk, chunk)],
            send_sem=tok_sem.at[0, i],
            recv_sem=tok_sem.at[1, i],
            device_id=sibling,
            device_id_type=GRID,
        )

    for i in range(2):
        swap(i).start()

    loads[2].wait()
    loads[3].wait()
    for i in range(T // chunk):
        rows = pl.ds(i * chunk, chunk)
        lg[rows, :] = jnp.dot(nrm[rows, :], wv[0], preferred_element_type=F32)
        lo[rows, :] = jnp.dot(nrm[rows, :], wv[1], preferred_element_type=F32)
    for i in range(T // chunk):
        swap(i).wait_recv()
        rows = pl.ds(T + i * chunk, chunk)
        lg[rows, :] = jnp.dot(nrm[rows, :], wv[0], preferred_element_type=F32)

    step_rows = 64

    def highest(i, best):
        rows = pl.ds(pl.multiple_of(i * step_rows, step_rows), step_rows)
        block = lg[rows, :].reshape(step_rows // 8, 8, H)
        return jnp.maximum(best, jnp.max(block, axis=0))

    best = lax.fori_loop(0, 2 * T // step_rows, highest, jnp.full((8, H), -jnp.inf, F32))
    column_max = jnp.max(best, axis=0, keepdims=True)

    def raise_rows(i, total):
        rows = pl.ds(pl.multiple_of(i * step_rows, step_rows), step_rows)
        raised = jnp.exp(lg[rows, :] - column_max)
        dsp[rows, :] = raised.astype(BF16)
        return total + jnp.sum(raised.reshape(step_rows // 8, 8, H), axis=0)

    total = lax.fori_loop(0, 2 * T // step_rows, raise_rows, jnp.zeros((8, H), F32))
    column_sum = jnp.sum(total, axis=0, keepdims=True)
    for j in range(H // LANES):
        cols = slice(j * LANES, (j + 1) * LANES)
        st[j, 0:1, :] = column_max[:, cols]
        st[j, 1:2, :] = column_sum[:, cols]

    def targets():
        for xh in range(xh_n):
            for yt in range(ny):
                for ct in range(2):
                    yield xh, yt, ct, (xh * ny + yt) * 2 + ct

    def to_owner(xh, yt, ct, number, h):
        xt = xh_n * c + xh
        row = number * R
        if h is None:
            src, dst = st.at[row // LANES], sr.at[me]
            ssem, rsem = st_send.at[number], st_recv.at[me]
        else:
            src, dst = part.at[pl.ds(row + h * half_rows, half_rows)], halves(rb, me, h)
            ssem, rsem = pb_send.at[number, h], pb_recv.at[me, h]
        here = (xt == x) & (yt == y) & (ct == c)
        far = pltpu.make_async_remote_copy(
            src_ref=src,
            dst_ref=dst,
            send_sem=ssem,
            recv_sem=rsem,
            device_id={"x": xt, "y": yt, "c": ct},
            device_id_type=GRID,
        )
        near = pltpu.make_async_copy(src, dst, rsem)
        return here, far, near

    def start_owner(*args):
        here, far, near = to_owner(*args)
        pl.when(jnp.logical_not(here))(far.start)
        pl.when(here)(near.start)

    for target in targets():
        start_owner(*target, None)

    block = ny * 2 * R
    for xh in range(xh_n):
        value = lax.dot_general(
            dsp[:, xh * block : (xh + 1) * block],
            nrm[...],
            (((0,), (0,)), ((), ())),
            preferred_element_type=F32,
        )
        part[xh * block : (xh + 1) * block, :] = value.astype(BF16)
        for target in targets():
            if target[0] == xh:
                start_owner(*target, 0)
    for target in targets():
        start_owner(*target, 1)

    def combine_rows(i, _):
        rows = pl.ds(pl.multiple_of(i * 32, 32), 32)
        one, two = lg[rows, :], lo[rows, :]
        top = jnp.maximum(
            jnp.max(one, axis=1, keepdims=True), jnp.max(two, axis=1, keepdims=True)
        )
        one, two = jnp.exp(one - top), jnp.exp(two - top)
        for k in range(xh_n):
            part_k = slice(k * block, (k + 1) * block)
            cb[xh_n * c + k, rows, :] = one[:, part_k].astype(BF16)
            cb[xh_n * (1 - c) + k, rows, :] = two[:, part_k].astype(BF16)
        weight = jnp.sum(one, axis=1, keepdims=True) + jnp.sum(two, axis=1, keepdims=True)
        rinv[rows, :] = jnp.broadcast_to(1.0 / weight, (32, LANES))
        return 0

    lax.fori_loop(0, T // 32, combine_rows, 0)

    def arrived(ref, sem):
        return pltpu.make_async_remote_copy(
            src_ref=ref,
            dst_ref=ref,
            send_sem=sem,
            recv_sem=sem,
            device_id=sibling,
            device_id_type=GRID,
        )

    for q in range(chips):
        arrived(sr.at[q], st_recv.at[q]).wait_recv()
    highs = [sr[q, 0:1, :] for q in range(chips)]
    peak = functools.reduce(jnp.maximum, highs)
    weights = [jnp.exp(t - peak) for t in highs]
    sums = functools.reduce(jnp.add, [w * sr[q, 1:2, :] for q, w in enumerate(weights)])
    vv[...] = jnp.zeros_like(vv)
    for q in range(chips):
        vv[q : q + 1, :] = weights[q] / sums
    vv[...] = jnp.transpose(vv[...])
    offset = lax.rem((lax.rem(x, xh_n) * ny + y) * 2 * R + c * R, LANES)

    def place(way, r):
        return 0 if r == 0 else way * kr + r

    def children(way, r):
        top = tops[way]
        return sorted((k for k in range(1, top + 1) if parent(k, top) == r), reverse=True)

    def pass_on(way, r, to, h):
        return pltpu.make_async_remote_copy(
            src_ref=halves(xin, place(way, r), h),
            dst_ref=halves(xin, place(way, to), h),
            send_sem=c_send.at[place(way, to), h],
            recv_sem=c_recv.at[place(way, to), h],
            device_id=along(way, to - r),
            device_id_type=GRID,
        )

    def owner_sum(h):
        rows = pl.ds(h * half_rows, half_rows)
        scale = vv[pl.ds(pl.multiple_of(offset + h * half_rows, half_rows), half_rows), :]
        acc = jnp.zeros((half_rows, D), F32)
        for q in range(chips):
            arrived(halves(rb, q, h), pb_recv.at[q, h]).wait_recv()
            acc = acc + scale[:, q : q + 1] * rb[q, rows, :].astype(F32)
        xin[0, rows, :] = acc.astype(BF16)
        forward(0, h)

    def forward(r, h):
        edges = [(to, way) for way in range(2) for to in children(way, r)]
        for to, way in sorted(edges, reverse=True):
            pass_on(way, r, to, h).start()

    def gather(r, h):
        for way in range(2):
            if r <= tops[way]:
                pass_on(way, parent(r, tops[way]), r, h).wait_recv()
                for to in children(way, r):
                    pass_on(way, r, to, h).start()

    def experts(first, h):
        spots = []
        for r in BATCHES[first]:
            if r <= kr:
                spots += [r, kr + r if r <= kl else 0]
        rows = pl.ds(h * half_rows, half_rows)
        blocks = [xin[spot, rows, :].astype(F32) for spot in spots]
        for i in range(E // 2):
            e = h * (E // 2) + i
            mine = slice(i * RE, (i + 1) * RE)
            lhs = jnp.concatenate([block[mine] for block in blocks], axis=0).astype(BF16)
            hidden = lax.dot_general(
                lhs, w1[e], (((1,), (1,)), ((), ())), preferred_element_type=F32
            )
            hidden = 0.5 * hidden * (1.0 + lax.erf(hidden * (0.5**0.5)))
            terms = jnp.dot(hidden.astype(BF16), w2[e], preferred_element_type=F32)
            for n, spot in enumerate(spots):
                tt[spot, pl.ds(e * RE, RE), :] = terms[n * RE : (n + 1) * RE]

    def hand_back(way, r, h):
        src, dst = ((dsl, drl), (dsr, drr))[way]
        return pltpu.make_async_remote_copy(
            src_ref=halves(src, r, h),
            dst_ref=halves(dst, r, h),
            send_sem=d_send.at[way, r, h],
            recv_sem=d_recv.at[way, r, h],
            device_id=along(1 - way, r - parent(r, tops[way])),
            device_id_type=GRID,
        )

    def summed(way, r, h, value):
        rows = pl.ds(h * half_rows, half_rows)
        for k in reversed(children(way, r)):
            hand_back(way, k, h).wait_recv()
            value = value + (drl, drr)[way][k, rows, :].astype(F32)
        return value

    def give_back(r, h):
        rows = pl.ds(h * half_rows, half_rows)
        for way in range(2):
            if r <= tops[way]:
                value = summed(way, r, h, tt[place(way, r), rows, :])
                (dsl, dsr)[way][r, rows, :] = value.astype(BF16)
                hand_back(way, r, h).start()

    own_place = pl.multiple_of((2 * me + c) * R, R)

    def result(h):
        value = tt[0, pl.ds(h * half_rows, half_rows), :]
        for way in range(2):
            value = summed(way, 0, h, value)
        start = pl.multiple_of(own_place + h * half_rows, half_rows)
        gg[pl.ds(start, half_rows), :] = value.astype(BF16)
        relay(me, h).start()

        def start_share(i, _):
            share(far_first(i), h).start()
            return 0

        lax.fori_loop(1, chips, start_share, 0)

    def half_of(q, core, h):
        return gg.at[pl.ds(pl.multiple_of((2 * q + core) * R + h * half_rows, half_rows), half_rows)]

    def share(j, h):
        dx, dy = j // ny, lax.rem(j, ny)
        ref = half_of(me, c, h)
        return pltpu.make_async_remote_copy(
            src_ref=ref,
            dst_ref=ref,
            send_sem=e_send.at[j, h],
            recv_sem=e_recv.at[me, h],
            device_id={"x": lax.rem(x + dx, nx), "y": lax.rem(y + dy, ny)},
            device_id_type=GRID,
        )

    def relay(q, h):
        ref = half_of(q, c, h)
        return pltpu.make_async_remote_copy(
            src_ref=ref,
            dst_ref=ref,
            send_sem=f_send.at[q, h],
            recv_sem=f_recv.at[q, h],
            device_id=sibling,
            device_id_type=GRID,
        )

    def far_first(i):
        dx = i // ny
        mid = nx // 2
        dx = jnp.where(dx < mid, dx, jnp.where(dx == nx - 1, mid, dx + 1))
        return dx * ny + lax.rem(i, ny)

    def from_chip(j):
        dx, dy = j // ny, lax.rem(j, ny)
        return lax.rem(x + nx - dx, nx) * ny + lax.rem(y + ny - dy, ny)

    def relay_row(row, h):
        def start_relay(i, _):
            q = from_chip(far_first(i))
            arrived(half_of(q, c, h), e_recv.at[q, h]).wait_recv()
            relay(q, h).start()
            return 0

        lax.fori_loop(max(1, row * ny), (row + 1) * ny, start_relay, 0)

    def row_came(row, h):
        def end_relay(i, _):
            q = from_chip(far_first(i))
            arrived(half_of(q, 1 - c, h), f_recv.at[q, h]).wait_recv()
            return 0

        lax.fori_loop(row * ny, (row + 1) * ny, end_relay, 0)

    loads[4].wait()
    loads[5].wait()
    acts = dict(
        B=lambda _, h: owner_sum(h),
        G=gather,
        X=experts,
        L=give_back,
        R=lambda _, h: result(h),
    )
    for step in ORDER:
        kind, h, r = step[0], int(step[1]), int(step[2:] or 0)
        if r <= kr:
            acts[kind](r, h)

    def mix(row, last_row):
        xt = lax.rem(x + nx - far_first(row * ny) // ny, nx)
        places = pl.ds(pl.multiple_of(xt * block, block), block)
        for i in range(T // chunk):
            rows = pl.ds(i * chunk, chunk)
            value = jnp.dot(cb[xt, rows, :], gg[places, :], preferred_element_type=F32)
            if row:
                value = value + total_out[rows, :]
            if last_row:
                outv[rows, :] = (value * rinv[rows, 0:1]).astype(BF16)
                write_out(i).start()
            else:
                total_out[rows, :] = value

    def write_out(i):
        rows = pl.ds(i * chunk, chunk)
        return pltpu.make_async_copy(outv.at[rows], mixed_hbm.at[rows], out_sem.at[i])

    for row in range(nx):
        for h in range(2):
            relay_row(row, h)
        if row:
            for h in range(2):
                row_came(row - 1, h)
            mix(row - 1, False)
    for h in range(2):
        row_came(nx - 1, h)
    mix(nx - 1, True)

    for i in range(2):
        swap(i).wait_send()
    for target in targets():
        for h in (None, 0, 1):
            here, far, near = to_owner(*target, h)
            pl.when(jnp.logical_not(here))(far.wait_send)
    for way in range(2):
        for r in range(1, tops[way] + 1):
            for h in range(2):
                pass_on(way, parent(r, tops[way]), r, h).wait_send()
                hand_back(way, r, h).wait_send()
    for h in range(2):

        def sent_share(j, _):
            share(j, h).wait_send()
            return 0

        def sent_relay(q, _):
            relay(q, h).wait_send()
            return 0

        lax.fori_loop(1, chips, sent_share, 0)
        lax.fori_loop(0, chips, sent_relay, 0)
    for i in range(T // chunk):
        write_out(i).wait()


def body(sizes, tokens, slot_weight, expert_in, expert_out):
    nz, nx, ny = sizes
    first = jnp.swapaxes(expert_in, 1, 2)
    T, D = tokens.shape
    S = slot_weight.shape[1]
    H = S // 2
    chips = nx * ny
    R = S // (2 * chips)
    E, FF = first.shape[:2]
    kr = nz // 2
    arrays = (tokens, slot_weight, first, expert_out)
    vmem = pltpu.VMEM
    dma = pltpu.SemaphoreType.DMA
    anywhere = pl.BlockSpec(memory_space=pl.ANY)
    return pl.pallas_call(
        functools.partial(layer, sizes),
        out_shape=jax.ShapeDtypeStruct((T, D), BF16),
        in_specs=[pl.BlockSpec(memory_space=pltpu.HBM)] * 4,
        out_specs=anywhere,
        scratch_shapes=[
            vmem((T, D), BF16),
            vmem((2, D, H), BF16),
            vmem((E, FF, D), BF16),
            vmem((E, FF, D), BF16),
            vmem((2 * T, D), BF16),
            vmem((2 * T, H), F32),
            vmem((T, H), F32),
            vmem((2 * T, H), BF16),
            vmem((H, D), BF16),
            vmem((H // LANES, 8, LANES), F32),
            vmem((chips, R, D), BF16),
            vmem((chips, 8, LANES), F32),
            vmem((LANES, LANES), F32),
            vmem((nz, R, D), BF16),
            vmem((nz, R, D), F32),
            vmem((kr + 1, R, D), BF16),
            vmem((kr + 1, R, D), BF16),
            vmem((kr + 1, R, D), BF16),
            vmem((kr + 1, R, D), BF16),
            vmem((S, D), BF16),
            vmem((nx, T, ny * 2 * R), BF16),
            vmem((T, LANES), F32),
            vmem((T, D), BF16),
            vmem((T, D), F32),
            dma((6,)),
            dma((2,)),
            dma((2, 2)),
            dma((chips,)),
            dma((chips,)),
            dma((chips, 2)),
            dma((chips, 2)),
            dma((nz, 2)),
            dma((nz, 2)),
            dma((2, kr + 1, 2)),
            dma((2, kr + 1, 2)),
            dma((chips, 2)),
            dma((chips, 2)),
            dma((chips, 2)),
            dma((chips, 2)),
        ],
        compiler_params=pltpu.CompilerParams(
            collective_id=0, has_side_effects=True, vmem_limit_bytes=28 * 2**20
        ),
        name="soft_moe",
    )(*(pltpu.with_memory_space_constraint(a, pltpu.HBM) for a in arrays))


def build(devices, sizes):
    nz, nx, ny = sizes
    torus = Mesh(devices.reshape(nz, nx, ny, 2), ("z", "x", "y", "c"))
    token = ("x", "y", "c")
    rows = ("z", "x", "y", "c")
    placed = (P(rows, None), P(), P(token, None, "z"), P(token, "z", None))
    return jax.shard_map(
        functools.partial(body, sizes),
        mesh=torus,
        in_specs=placed,
        out_specs=P(rows, None),
        check_vma=False,
    )


def solution(mesh):
    return build(mesh.devices, (mesh.shape["batch"], 4, 4))
```
